32 devices in a mesh: beam: 8 (over z, y), elem: 4 (over x, core).
Axes of the slice: x: 2, y: 2, z: 4, core: 2. Of those that a mesh axis runs over, the one named last changes fastest.
Arguments:
- signals: bfloat16 [2, 16384, 256], P(None, 'elem', 'beam'), may hold values from -6 to 6
- weights: bfloat16 [2, 16384, 16384], P(None, 'beam', 'elem'), may hold values from -0.0625 to 0.0625
- element_flags: int32 [16384], P('elem'), may hold values from 0 to 1, as said below
Outputs:
- beam_out: bfloat16 [2, 16384, 256], P(None, ('beam', 'elem'))
- beam_power: float32 [16384], P(('beam', 'elem'))
The draws below stay inside these ranges and needn't reach their ends.
Inputs may be any that keep to these rules, and one draw needn't show every extreme that they name: `element_flags`: element 16384 - 1 is always live.
All inputs are finite; a program needn't handle non-finite values.
Results may differ from the reference program's by a relative error of at most 0.001.
Values may be sent and summed in bfloat16 or wider, within the bound.
A program may use at most 128 MiB of HBM per device.

```python
import jax
import jax.numpy as jnp
from jax import lax

B = 16384
E = 16384
T_SIZE = 256


def draw_element_flags(key, part):
    positions = jnp.arange(E, dtype=jnp.int32)
    levels = jax.random.randint(key, (E,), 0, 1000, dtype=jnp.int32)
    threshold = 300 + 650 * positions // E
    alive = (levels < threshold) | (positions == E - 1)
    return alive.astype(jnp.int32)


def strengthened(array, rng, source, target, shards_of, factor):
    def block_of(axis_at):
        return (jnp.arange(array.shape[axis_at]) // (array.shape[axis_at] // shards_of)).reshape((-1,) + (1,) * (array.ndim - 1 - axis_at))

    one_side = jax.random.permutation(rng, shards_of)[block_of(target)]
    far = (block_of(target) + shards_of // 2) % shards_of
    return jnp.where((block_of(source) == one_side) | (block_of(source) == far), factor * array, array)


def steps_of(own_key, shape, split, least, top_value):
    gain, own = 1.0, jax.random.fold_in(own_key, 6)
    for position, blocks in split:
        heights = jnp.exp(jax.random.uniform(jax.random.fold_in(own, position), (blocks,), jnp.float32, least / len(split), top_value / len(split)))
        gain = gain * jnp.repeat(heights, shape[position] // blocks).reshape([-1 if axis == position else 1 for axis in range(len(shape))])
    return gain


def bell_draw(rng, extent, scale, most, split=(), kind=jnp.bfloat16):
    array = jax.random.normal(rng, extent, jnp.float32) * scale
    if len(split) > 0:
        array = steps_of(rng, extent, split, -0.22, 0.18) * array
    return jnp.clip(array, min=-most, max=most).astype(kind)


def gaussian_with(rng, extent, width, reach, shards, heavy, kind=jnp.bfloat16):
    array = width * jax.random.normal(rng, extent, jnp.float32)
    if shards:
        array = array * steps_of(rng, extent, shards, -0.22, 0.18)
    return jnp.clip(strengthened(array, jax.random.fold_in(rng, 3), *heavy), -reach, reach).astype(kind)


def setup_inputs(seed: int = 0) -> dict:
    keys = jax.random.split(jax.random.key(seed), 4)
    return {
        "signals": bell_draw(keys[0], (2, E, T_SIZE), 1.0, 6.0, ((1, 4), (2, 8))),
        "weights": gaussian_with(keys[1], (2, B, E), E ** -0.5, 0.0625, ((1, 8), (2, 4)), (2, 1, 8, 2.0)),
        "element_flags": draw_element_flags(jax.random.fold_in(keys[3], 71), 0),
    }


def reference(signals, weights, element_flags):
    masked = signals * element_flags.astype(jnp.bfloat16)[None, :, None]
    live_total = jnp.sum(element_flags.astype(jnp.float32))
    beam_gain = jnp.sqrt(jnp.float32(E) / live_total)
    real_part = jnp.dot(weights[0], masked[0], preferred_element_type=jnp.float32) - jnp.dot(weights[1], masked[1], preferred_element_type=jnp.float32)
    imag_part = jnp.dot(weights[0], masked[1], preferred_element_type=jnp.float32) + jnp.dot(weights[1], masked[0], preferred_element_type=jnp.float32)
    scaled = jnp.stack([real_part, imag_part]) * beam_gain
    beam_out = scaled.astype(jnp.bfloat16)
    beam_power = lax.optimization_barrier(jnp.mean(scaled[0] * scaled[0] + scaled[1] * scaled[1], axis=1))
    return (beam_out, beam_power)
```

```python
import functools

import jax
import jax.numpy as jnp
from jax import lax
from jax.experimental import pallas as pl
from jax.experimental.pallas import tpu as pltpu
from jax.sharding import PartitionSpec as P

PIECES = 4
LANES = 128
MESH = pl.DeviceIdType.MESH


def ring_order(mesh):
    nb = mesh.shape["beam"]
    try:
        coords = [tuple(d.coords) for d in mesh.devices[:, 0]]
    except AttributeError:
        return list(range(nb))
    axes = [a for a in range(len(coords[0])) if len({c[a] for c in coords}) > 1]
    if len(axes) != 2:
        return list(range(nb))
    values = [sorted({c[a] for c in coords}) for a in axes]
    if len(values[0]) % 2:
        axes, values = axes[::-1], values[::-1]
    rows, cols = len(values[0]), len(values[1])
    if rows % 2 or rows * cols != nb:
        return list(range(nb))
    at = {(values[0].index(c[axes[0]]), values[1].index(c[axes[1]])): i for i, c in enumerate(coords)}
    path = [(0, 0)]
    for r in range(rows):
        inner = range(1, cols) if r % 2 == 0 else range(cols - 1, 0, -1)
        path += [(r, c) for c in inner]
    path += [(r, 0) for r in range(rows - 1, 0, -1)]
    return [at[p] for p in path]


def lookup(table, index):
    value = jnp.int32(table[0])
    for i in range(1, len(table)):
        value = jnp.where(index == i, jnp.int32(table[i]), value)
    return value


def kernel(order, ne, elements, s_ref, cnt_ref, w_ref, out_ref, pow_ref,
           blocks, weights, rhs, part, first, second, counts,
           ring_send, ring_recv, w_sem, s_sem, first_send, first_recv, second_send, second_recv,
           cnt_send, cnt_recv, cnt_sem):
    nb = len(order)
    half = nb // 2
    q, two_t, kq = s_ref.shape
    tb = two_t // 2
    chunks, _, mo, width = part.shape
    group = width // two_t
    ways = ne // 2
    snaps = nb * tb

    me_b = lax.axis_index("beam")
    me_e = lax.axis_index("elem")
    inverse = [order.index(i) for i in range(nb)]
    pos = lookup(inverse, me_b)
    ahead = lookup([order[(inverse[i] + 1) % nb] for i in range(nb)], me_b)
    behind = lookup([order[(inverse[i] - 1) % nb] for i in range(nb)], me_b)
    core = lax.rem(me_e, 2)
    mine = me_e // 2
    partner = me_e + 1 - 2 * core

    def slot_of(way, d):
        return d if (way == 0 or d in (0, half)) else half + d

    arrivals = [[(d, j) for d in range(1, half) for j in range(q)]
                + [(half, j) for j in (range(q // 2) if way == 0 else range(q // 2, q))]
                for way in (0, 1)]
    number = [{item: k for k, item in enumerate(a)} for a in arrivals]

    def ring_copy(way, d, j):
        k = number[way][(d, j)]
        return pltpu.make_async_remote_copy(
            src_ref=blocks.at[slot_of(way, d - 1), j],
            dst_ref=blocks.at[slot_of(way, d), j],
            send_sem=ring_send.at[way, k], recv_sem=ring_recv.at[way, k],
            device_id={"beam": ahead if way == 0 else behind}, device_id_type=MESH)

    def weight_copy(i, j):
        return pltpu.make_async_copy(
            w_ref.at[i, :, pl.ds(j * kq, kq)], weights.at[j, :, pl.ds(i * kq, kq)], w_sem.at[i, j])

    def count_copy(r):
        return pltpu.make_async_remote_copy(
            src_ref=cnt_ref, dst_ref=counts.at[r], send_sem=cnt_send.at[r - 1], recv_sem=cnt_recv.at[r - 1],
            device_id={"elem": lax.rem(me_e + r, ne)}, device_id_type=MESH)

    def kept(i):
        return 2 * lax.rem(mine + i, ways) + core

    def given(i):
        return 2 * lax.rem(mine + i, ways) + 1 - core

    def first_copy(c, i):
        return pltpu.make_async_remote_copy(
            src_ref=part.at[c, given(i)], dst_ref=first.at[c, i],
            send_sem=first_send.at[c, i], recv_sem=first_recv.at[c, i],
            device_id={"elem": partner}, device_id_type=MESH)

    def second_copy(c, i):
        return pltpu.make_async_remote_copy(
            src_ref=first.at[c, i], dst_ref=second.at[c, i - 1],
            send_sem=second_send.at[c, i - 1], recv_sem=second_recv.at[c, i - 1],
            device_id={"elem": kept(i)}, device_id_type=MESH)

    own_in = pltpu.make_async_copy(s_ref, blocks.at[0], s_sem)
    own_in.start()
    own_cnt = pltpu.make_async_copy(cnt_ref, counts.at[0], cnt_sem)
    own_cnt.start()

    barrier = pltpu.get_barrier_semaphore()
    for b in (ahead, behind):
        pl.semaphore_signal(barrier, inc=1, device_id={"beam": b}, device_id_type=MESH)
    for r in range(1, ne):
        pl.semaphore_signal(barrier, inc=1, device_id={"elem": lax.rem(me_e + r, ne)}, device_id_type=MESH)
    pl.semaphore_wait(barrier, 2 + ne - 1)

    own_in.wait()
    for j in range(q):
        for way in (0, 1):
            if (1, j) in number[way]:
                ring_copy(way, 1, j).start()
    for r in range(1, ne):
        count_copy(r).start()
    for j in range(q):
        for i in (0, 1):
            weight_copy(i, j).start()

    sequence = [(0, 0)]
    for d in range(1, half):
        sequence += [(0, d), (1, d)]
    sequence += [(0, half)]

    def members(c):
        return sequence[c * group:(c + 1) * group]

    def stage(c, j):
        for s, (way, d) in enumerate(members(c)):
            re = blocks[slot_of(way, d), j, :tb, :]
            im = blocks[slot_of(way, d), j, tb:, :]
            lo, hi = s * tb, (group + s) * tb
            rhs[lo:lo + tb, :kq] = re
            rhs[hi:hi + tb, :kq] = im
            rhs[lo:lo + tb, kq:] = -im
            rhs[hi:hi + tb, kq:] = re

    def multiply(c, j, o, fresh):
        rows = pl.ds(pl.multiple_of(o * mo, mo), mo)
        product = lax.dot_general(weights[j, rows, :], rhs[...], (((1,), (1,)), ((), ())),
                                  preferred_element_type=jnp.float32)
        if fresh:
            part[c, o] = product
        else:
            part[c, o] += product

    pieces_done = [0] * chunks
    weights_here = set()
    waiting = []

    def pass_on(c):
        for i in range(1, ways):
            first_copy(c, i).wait_recv()
            first[c, i] += part[c, kept(i)]
            second_copy(c, i).start()

    def piece(c, j):
        stage(c, j)
        if j not in weights_here:
            weights_here.add(j)
            for i in (0, 1):
                weight_copy(i, j).wait()
        fresh = pieces_done[c] == 0
        pieces_done[c] += 1
        if pieces_done[c] < q:
            @pl.loop(0, ne)
            def _(o):
                multiply(c, j, o, fresh)
            return
        for i in list(range(1, ways)) + [0]:
            multiply(c, j, given(i), fresh)
            first_copy(c, i).start()
        for i in range(1, ways):
            multiply(c, j, kept(i), fresh)
            if c == chunks - 1:
                first_copy(c, i).wait_recv()
                first[c, i] += part[c, kept(i)]
                second_copy(c, i).start()
        multiply(c, j, kept(0), fresh)
        if c < chunks - 1:
            waiting.append(c)

    arrived = {((0, 0), j) for j in range(q)}
    todo = [(c, j) for c in range(chunks) for j in range(q)]

    def run_ready():
        for c, j in list(todo):
            if all((m, j) in arrived for m in members(c)):
                todo.remove((c, j))
                piece(c, j)

    for k in range(len(arrivals[0])):
        for way in (0, 1):
            d, j = arrivals[way][k]
            ring_copy(way, d, j).wait_recv()
            if (d + 1, j) in number[way]:
                ring_copy(way, d + 1, j).start()
            arrived.add(((0 if d == half else way, d), j))
        for c in waiting:
            pass_on(c)
        waiting.clear()
        run_ready()
    for c in waiting:
        pass_on(c)
    waiting.clear()

    own_cnt.wait()
    total = counts[0]
    for r in range(1, ne):
        count_copy(r).wait()
        total = total + counts[r]
    gain = jnp.sqrt(jnp.float32(elements) / total)[0:1, 0:1]

    square = jnp.zeros((mo, width), jnp.float32)
    moved = jnp.zeros((mo, 2 * snaps), jnp.float32)
    for c in range(chunks):
        first_copy(c, 0).wait_recv()
        value = part[c, me_e] + first[c, 0]
        for i in range(1, ways):
            second_copy(c, i).wait_recv()
            value = value + second[c, i - 1]
        value = value * gain
        square = square + value * value
        column = lax.broadcasted_iota(jnp.int32, (width, 2 * snaps), 0)
        target = lax.broadcasted_iota(jnp.int32, (width, 2 * snaps), 1)
        wanted = column
        for s, (way, d) in enumerate(members(c)):
            source = lookup(order, lax.rem(pos + (d if way else nb - d), nb))
            for p in (0, 1):
                lo = (p * group + s) * tb
                inside = (column >= lo) & (column < lo + tb)
                wanted = jnp.where(inside, column - lo + p * snaps + source * tb, wanted)
        select = jnp.where(wanted == target, 1.0, 0.0).astype(jnp.bfloat16)
        moved = moved + jnp.dot(value.astype(jnp.bfloat16), select, preferred_element_type=jnp.float32)
    moved = moved.astype(jnp.bfloat16)
    out_ref[0] = moved[:, :snaps]
    out_ref[1] = moved[:, snaps:]
    power = jnp.sum(square, axis=1, keepdims=True) * (1.0 / snaps)
    pow_ref[...] = jnp.broadcast_to(power, pow_ref.shape)

    for way in (0, 1):
        for d, j in arrivals[way]:
            ring_copy(way, d, j).wait_send()
    for c in range(chunks):
        for i in range(ways):
            first_copy(c, i).wait_send()
        for i in range(1, ways):
            second_copy(c, i).wait_send()


def body(order, ne, signals, weights, element_flags):
    nb = len(order)
    _, depth, tb = signals.shape
    rows = weights.shape[1]
    mo = rows // ne
    q = PIECES
    kq = depth // q
    group = min(nb, max(1, LANES // tb))
    chunks = nb // group
    width = 2 * group * tb
    ways = ne // 2
    items = q * (nb // 2) - q // 2
    masked = signals * element_flags.astype(jnp.bfloat16)[None, :, None]
    sent = masked.reshape(2, q, kq, tb).transpose(1, 0, 3, 2).reshape(q, 2 * tb, kq)
    count = jnp.broadcast_to(jnp.sum(element_flags.astype(jnp.float32)), (8, LANES))
    dma = pltpu.SemaphoreType.DMA
    anywhere = pl.BlockSpec(memory_space=pl.ANY)
    vmem = pl.BlockSpec(memory_space=pltpu.VMEM)
    out, power = pl.pallas_call(
        functools.partial(kernel, order, ne, depth * ne),
        out_shape=(jax.ShapeDtypeStruct((2, mo, nb * tb), jnp.bfloat16),
                   jax.ShapeDtypeStruct((mo, LANES), jnp.float32)),
        in_specs=[anywhere, anywhere, anywhere],
        out_specs=(vmem, vmem),
        scratch_shapes=[
            pltpu.VMEM((nb, q, 2 * tb, kq), jnp.bfloat16),
            pltpu.VMEM((q, rows, 2 * kq), jnp.bfloat16),
            pltpu.VMEM((width, 2 * kq), jnp.bfloat16),
            pltpu.VMEM((chunks, ne, mo, width), jnp.float32),
            pltpu.VMEM((chunks, ways, mo, width), jnp.float32),
            pltpu.VMEM((chunks, max(1, ways - 1), mo, width), jnp.float32),
            pltpu.VMEM((ne, 8, LANES), jnp.float32),
            dma((2, items)), dma((2, items)), dma((2, q)), dma,
            dma((chunks, ways)), dma((chunks, ways)),
            dma((chunks, max(1, ways - 1))), dma((chunks, max(1, ways - 1))),
            dma((ne - 1,)), dma((ne - 1,)), dma,
        ],
        compiler_params=pltpu.CompilerParams(
            collective_id=0, has_side_effects=True, vmem_limit_bytes=60 * 2**20),
        name="beamform",
    )(sent, count, weights)
    return out, power[:, 0]


def solution(mesh):
    return jax.shard_map(
        functools.partial(body, ring_order(mesh), mesh.shape["elem"]),
        mesh=mesh,
        in_specs=(P(None, "elem", "beam"), P(None, "beam", "elem"), P("elem")),
        out_specs=(P(None, ("beam", "elem"), None), P(("beam", "elem"))),
        check_vma=False,
    )
```

```python
import functools

import jax
import jax.numpy as jnp
from jax import lax
from jax.experimental import pallas as pl
from jax.experimental.pallas import tpu as pltpu
from jax.sharding import PartitionSpec as P

PIECES = 4
LANES = 128
MESH = pl.DeviceIdType.MESH


def ring_order(mesh):
    nb = mesh.shape["beam"]
    try:
        coords = [tuple(d.coords) for d in mesh.devices[:, 0]]
    except AttributeError:
        return list(range(nb))
    axes = [a for a in range(len(coords[0])) if len({c[a] for c in coords}) > 1]
    if len(axes) != 2:
        return list(range(nb))
    values = [sorted({c[a] for c in coords}) for a in axes]
    if len(values[0]) % 2:
        axes, values = axes[::-1], values[::-1]
    rows, cols = len(values[0]), len(values[1])
    if rows % 2 or rows * cols != nb:
        return list(range(nb))
    at = {(values[0].index(c[axes[0]]), values[1].index(c[axes[1]])): i for i, c in enumerate(coords)}
    path = [(0, 0)]
    for r in range(rows):
        inner = range(1, cols) if r % 2 == 0 else range(cols - 1, 0, -1)
        path += [(r, c) for c in inner]
    path += [(r, 0) for r in range(rows - 1, 0, -1)]
    return [at[p] for p in path]


def lookup(table, index):
    value = jnp.int32(table[0])
    for i in range(1, len(table)):
        value = jnp.where(index == i, jnp.int32(table[i]), value)
    return value


def kernel(order, ne, s_ref, flag_ref, w_ref, out_ref, pow_ref,
           blocks, mask, weights, rhs, part, first, second, counts,
           ring_send, ring_recv, w_sem, s_sem, first_send, first_recv, second_send, second_recv,
           cnt_send, cnt_recv):
    nb = len(order)
    half = nb // 2
    _, tb, depth = s_ref.shape
    q = PIECES
    two_t, kq = 2 * tb, depth // q
    chunks, _, mo, width = part.shape
    group = width // two_t
    ways = ne // 2
    snaps = nb * tb

    me_b = lax.axis_index("beam")
    me_e = lax.axis_index("elem")
    inverse = [order.index(i) for i in range(nb)]
    pos = lookup(inverse, me_b)
    ahead = lookup([order[(inverse[i] + 1) % nb] for i in range(nb)], me_b)
    behind = lookup([order[(inverse[i] - 1) % nb] for i in range(nb)], me_b)
    core = lax.rem(me_e, 2)
    mine = me_e // 2
    partner = me_e + 1 - 2 * core

    def slot_of(way, d):
        return d if (way == 0 or d in (0, half)) else half + d

    last = (((half - 1, 0), (half - 1, 1), (half, 0), (half - 1, 2), (half, 1), (half - 1, 3)),
            ((half - 1, 2), (half - 1, 3), (half - 1, 0), (half, 2), (half - 1, 1), (half, 3)))
    arrivals = [[(d, j) for d in range(1, half - 1) for j in range(q)]
                + [(d, j) for d, j in last[way] if d > 0] for way in (0, 1)]
    number = [{item: k for k, item in enumerate(a)} for a in arrivals]

    def ring_copy(way, d, j):
        k = number[way][(d, j)]
        return pltpu.make_async_remote_copy(
            src_ref=(s_ref if d == 1 else blocks.at[slot_of(way, d - 1)]).at[:, :, pl.ds(j * kq, kq)],
            dst_ref=blocks.at[slot_of(way, d), :, :, pl.ds(j * kq, kq)],
            send_sem=ring_send.at[way, k], recv_sem=ring_recv.at[way, k],
            device_id={"beam": ahead if way == 0 else behind}, device_id_type=MESH)

    def weight_copy(i, j):
        return pltpu.make_async_copy(
            w_ref.at[i, :, pl.ds(j * kq, kq)], weights.at[j, :, pl.ds(i * kq, kq)], w_sem.at[i, j])

    def count_copy(r):
        return pltpu.make_async_remote_copy(
            src_ref=flag_ref, dst_ref=counts.at[r - 1], send_sem=cnt_send.at[r - 1], recv_sem=cnt_recv.at[r - 1],
            device_id={"elem": lax.rem(me_e + r, ne)}, device_id_type=MESH)

    def kept(i):
        return 2 * lax.rem(mine + i, ways) + core

    def given(i):
        return 2 * lax.rem(mine + i, ways) + 1 - core

    def first_copy(c, i):
        return pltpu.make_async_remote_copy(
            src_ref=part.at[c, given(i)], dst_ref=first.at[c, i],
            send_sem=first_send.at[c, i], recv_sem=first_recv.at[c, i],
            device_id={"elem": partner}, device_id_type=MESH)

    def second_copy(c, i):
        return pltpu.make_async_remote_copy(
            src_ref=first.at[c, i], dst_ref=second.at[c, i - 1],
            send_sem=second_send.at[c, i - 1], recv_sem=second_recv.at[c, i - 1],
            device_id={"elem": kept(i)}, device_id_type=MESH)

    own_in = pltpu.make_async_copy(s_ref, blocks.at[0], s_sem)
    own_in.start()

    barrier = pltpu.get_barrier_semaphore()
    for b in (ahead, behind):
        pl.semaphore_signal(barrier, inc=1, device_id={"beam": b}, device_id_type=MESH)
    for r in range(1, ne):
        pl.semaphore_signal(barrier, inc=1, device_id={"elem": lax.rem(me_e + r, ne)}, device_id_type=MESH)
    pl.semaphore_wait(barrier, 2 + ne - 1)

    arrived = {((0, 0), j) for j in range(q)}
    sent = [0, 0]

    def send_ready():
        for way in (0, 1):
            while sent[way] < len(arrivals[way]):
                d, j = arrivals[way][sent[way]]
                if d > 1 and ((way, d - 1), j) not in arrived:
                    break
                ring_copy(way, d, j).start()
                sent[way] += 1

    send_ready()
    for r in range(1, ne):
        count_copy(r).start()
    for j in range(q):
        for i in (0, 1):
            weight_copy(i, j).start()

    mask[...] = jnp.broadcast_to(flag_ref[...].astype(jnp.float32).astype(jnp.bfloat16), mask.shape)
    own_in.wait()

    sequence = [(0, 0)]
    for d in range(1, half):
        sequence += [(0, d), (1, d)]
    sequence += [(0, half)]

    def members(c):
        return sequence[c * group:(c + 1) * group]

    def stage(c, j):
        for s, (way, d) in enumerate(members(c)):
            columns = pl.ds(j * kq, kq)
            re = blocks[slot_of(way, d), 0, :, columns] * mask[:, columns]
            im = blocks[slot_of(way, d), 1, :, columns] * mask[:, columns]
            lo, hi = s * tb, (group + s) * tb
            rhs[lo:lo + tb, :kq] = re
            rhs[hi:hi + tb, :kq] = im
            rhs[lo:lo + tb, kq:] = -im
            rhs[hi:hi + tb, kq:] = re

    def multiply(c, j, o, fresh):
        rows = pl.ds(pl.multiple_of(o * mo, mo), mo)
        product = lax.dot_general(weights[j, rows, :], rhs[...], (((1,), (1,)), ((), ())),
                                  preferred_element_type=jnp.float32)
        if fresh:
            part[c, o] = product
        else:
            part[c, o] += product

    pieces_done = [0] * chunks
    weights_here = set()
    waiting = []

    def pass_on(c):
        for i in range(1, ways):
            first_copy(c, i).wait_recv()
            first[c, i] += part[c, kept(i)]
            second_copy(c, i).start()

    def piece(c, j):
        stage(c, j)
        if j not in weights_here:
            weights_here.add(j)
            for i in (0, 1):
                weight_copy(i, j).wait()
        fresh = pieces_done[c] == 0
        pieces_done[c] += 1
        if pieces_done[c] < q:
            @pl.loop(0, ne)
            def _(o):
                multiply(c, j, o, fresh)
            return
        for i in list(range(1, ways)) + [0]:
            multiply(c, j, given(i), fresh)
            first_copy(c, i).start()
        for i in range(1, ways):
            multiply(c, j, kept(i), fresh)
            if c == chunks - 1:
                first_copy(c, i).wait_recv()
                first[c, i] += part[c, kept(i)]
                second_copy(c, i).start()
        multiply(c, j, kept(0), fresh)
        if c < chunks - 1:
            waiting.append(c)

    todo = [(c, j) for c in range(chunks) for j in range(q)]

    def run_ready():
        for c, j in list(todo):
            if all((m, j) in arrived for m in members(c)):
                todo.remove((c, j))
                piece(c, j)

    for k in range(len(arrivals[0])):
        for way in (0, 1):
            d, j = arrivals[way][k]
            ring_copy(way, d, j).wait_recv()
            arrived.add(((0 if d == half else way, d), j))
            send_ready()
        for c in waiting:
            pass_on(c)
        waiting.clear()
        run_ready()
    for c in waiting:
        pass_on(c)
    waiting.clear()

    live = flag_ref[...].astype(jnp.float32)
    for r in range(1, ne):
        count_copy(r).wait()
        live = live + counts[r - 1].astype(jnp.float32)
    gain = jnp.sqrt(jnp.float32(depth * ne) / jnp.sum(live, axis=1, keepdims=True))

    square = jnp.zeros((mo, width), jnp.float32)
    moved = jnp.zeros((mo, 2 * snaps), jnp.float32)
    for c in range(chunks):
        first_copy(c, 0).wait_recv()
        value = part[c, me_e] + first[c, 0]
        for i in range(1, ways):
            second_copy(c, i).wait_recv()
            value = value + second[c, i - 1]
        value = value * gain
        square = square + value * value
        column = lax.broadcasted_iota(jnp.int32, (width, 2 * snaps), 0)
        target = lax.broadcasted_iota(jnp.int32, (width, 2 * snaps), 1)
        wanted = column
        for s, (way, d) in enumerate(members(c)):
            source = lookup(order, lax.rem(pos + (d if way else nb - d), nb))
            for p in (0, 1):
                lo = (p * group + s) * tb
                inside = (column >= lo) & (column < lo + tb)
                wanted = jnp.where(inside, column - lo + p * snaps + source * tb, wanted)
        select = jnp.where(wanted == target, 1.0, 0.0).astype(jnp.bfloat16)
        moved = moved + jnp.dot(value.astype(jnp.bfloat16), select, preferred_element_type=jnp.float32)
    moved = moved.astype(jnp.bfloat16)
    out_ref[0] = moved[:, :snaps]
    out_ref[1] = moved[:, snaps:]
    power = jnp.sum(square, axis=1, keepdims=True) * (1.0 / snaps)
    pow_ref[...] = jnp.broadcast_to(power, (mo, LANES)).T[0:1, :]

    for way in (0, 1):
        for d, j in arrivals[way]:
            ring_copy(way, d, j).wait_send()
    for c in range(chunks):
        for i in range(ways):
            first_copy(c, i).wait_send()
        for i in range(1, ways):
            second_copy(c, i).wait_send()


def body(order, ne, signals, weights, element_flags):
    nb = len(order)
    _, depth, tb = signals.shape
    rows = weights.shape[1]
    mo = rows // ne
    q = PIECES
    kq = depth // q
    group = min(nb, max(1, LANES // tb))
    chunks = nb // group
    width = 2 * group * tb
    ways = ne // 2
    items = q * (nb // 2) - q // 2
    dma = pltpu.SemaphoreType.DMA
    anywhere = pl.BlockSpec(memory_space=pl.ANY)
    vmem = pl.BlockSpec(memory_space=pltpu.VMEM)
    out, power = pl.pallas_call(
        functools.partial(kernel, order, ne),
        out_shape=(jax.ShapeDtypeStruct((2, mo, nb * tb), jnp.bfloat16),
                   jax.ShapeDtypeStruct((1, mo), jnp.float32)),
        in_specs=[anywhere, vmem, anywhere],
        out_specs=(vmem, vmem),
        scratch_shapes=[
            pltpu.VMEM((nb, 2, tb, depth), jnp.bfloat16),
            pltpu.VMEM((tb, depth), jnp.bfloat16),
            pltpu.VMEM((q, rows, 2 * kq), jnp.bfloat16),
            pltpu.VMEM((width, 2 * kq), jnp.bfloat16),
            pltpu.VMEM((chunks, ne, mo, width), jnp.float32),
            pltpu.VMEM((chunks, ways, mo, width), jnp.float32),
            pltpu.VMEM((chunks, max(1, ways - 1), mo, width), jnp.float32),
            pltpu.VMEM((ne - 1, 1, depth), jnp.int32),
            dma((2, items)), dma((2, items)), dma((2, q)), dma,
            dma((chunks, ways)), dma((chunks, ways)),
            dma((chunks, max(1, ways - 1))), dma((chunks, max(1, ways - 1))),
            dma((ne - 1,)), dma((ne - 1,)),
        ],
        compiler_params=pltpu.CompilerParams(
            collective_id=0, has_side_effects=True, vmem_limit_bytes=60 * 2**20),
        name="beamform",
    )(signals.transpose(0, 2, 1), element_flags.reshape(1, depth), weights)
    return out, power.reshape(mo)


def solution(mesh):
    return jax.shard_map(
        functools.partial(body, ring_order(mesh), mesh.shape["elem"]),
        mesh=mesh,
        in_specs=(P(None, "elem", "beam"), P(None, "beam", "elem"), P("elem")),
        out_specs=(P(None, ("beam", "elem"), None), P(("beam", "elem"))),
        check_vma=False,
    )
```

```python
import functools

import jax
import jax.numpy as jnp
from jax import lax
from jax.experimental import pallas as pl
from jax.experimental.pallas import tpu as pltpu
from jax.sharding import PartitionSpec as P

PIECES = 4
LANES = 128
SPLIT = 2
MESH = pl.DeviceIdType.MESH


def ring_order(mesh):
    nb = mesh.shape["beam"]
    try:
        coords = [tuple(d.coords) for d in mesh.devices[:, 0]]
    except AttributeError:
        return list(range(nb))
    axes = [a for a in range(len(coords[0])) if len({c[a] for c in coords}) > 1]
    if len(axes) != 2:
        return list(range(nb))
    values = [sorted({c[a] for c in coords}) for a in axes]
    if len(values[0]) % 2:
        axes, values = axes[::-1], values[::-1]
    rows, cols = len(values[0]), len(values[1])
    if rows % 2 or rows * cols != nb:
        return list(range(nb))
    at = {(values[0].index(c[axes[0]]), values[1].index(c[axes[1]])): i for i, c in enumerate(coords)}
    path = [(0, 0)]
    for r in range(rows):
        inner = range(1, cols) if r % 2 == 0 else range(cols - 1, 0, -1)
        path += [(r, c) for c in inner]
    path += [(r, 0) for r in range(rows - 1, 0, -1)]
    return [at[p] for p in path]


def lookup(table, index):
    value = jnp.int32(table[0])
    for i in range(1, len(table)):
        value = jnp.where(index == i, jnp.int32(table[i]), value)
    return value


def kernel(order, ne, s_ref, flag_ref, w_ref, out_ref, pow_ref,
           blocks, mask, weights, rhs, part, first, second, counts,
           ring_send, ring_recv, w_sem, s_sem, first_send, first_recv, second_send, second_recv,
           cnt_send, cnt_recv):
    nb = len(order)
    half = nb // 2
    _, tb, depth = s_ref.shape
    q = PIECES
    two_t, kq = 2 * tb, depth // q
    chunks, _, mo, width = part.shape
    group = width // two_t
    ways = ne // 2
    snaps = nb * tb

    me_b = lax.axis_index("beam")
    me_e = lax.axis_index("elem")
    inverse = [order.index(i) for i in range(nb)]
    pos = lookup(inverse, me_b)
    ahead = lookup([order[(inverse[i] + 1) % nb] for i in range(nb)], me_b)
    behind = lookup([order[(inverse[i] - 1) % nb] for i in range(nb)], me_b)
    core = lax.rem(me_e, 2)
    mine = me_e // 2
    partner = me_e + 1 - 2 * core

    def slot_of(way, d):
        return d if (way == 0 or d in (0, half)) else half + d

    if half == 4:
        arrivals = [[(1, 0), (1, 1), (2, 0), (1, 2), (2, 1), (1, 3), (2, 2), (2, 3),
                     (3, 0), (3, 1), (3, 2), (3, 3), (4, 2), (4, 3)],
                    [(1, 0), (1, 1), (2, 0), (1, 2), (3, 0), (1, 3), (2, 1), (4, 0),
                     (3, 1), (2, 2), (4, 1), (2, 3), (3, 2), (3, 3)]]
    else:
        last = (((half - 1, 0), (half - 1, 1), (half - 1, 2), (half - 1, 3), (half, 2), (half, 3)),
                ((half - 1, 0), (half - 1, 1), (half, 0), (half - 1, 2), (half, 1), (half - 1, 3)))
        arrivals = [[(d, j) for d in range(1, half - 1) for j in range(q)]
                    + [(d, j) for d, j in last[way] if d > 0] for way in (0, 1)]
    number = [{item: k for k, item in enumerate(a)} for a in arrivals]

    def ring_copy(way, d, j):
        k = number[way][(d, j)]
        return pltpu.make_async_remote_copy(
            src_ref=(s_ref if d == 1 else blocks.at[slot_of(way, d - 1)]).at[:, :, pl.ds(j * kq, kq)],
            dst_ref=blocks.at[slot_of(way, d), :, :, pl.ds(j * kq, kq)],
            send_sem=ring_send.at[way, k], recv_sem=ring_recv.at[way, k],
            device_id={"beam": ahead if way == 0 else behind}, device_id_type=MESH)

    def weight_copy(i, j):
        return pltpu.make_async_copy(
            w_ref.at[i, :, pl.ds(j * kq, kq)], weights.at[j, :, pl.ds(i * kq, kq)], w_sem.at[i, j])

    def count_copy(r):
        return pltpu.make_async_remote_copy(
            src_ref=flag_ref, dst_ref=counts.at[r - 1], send_sem=cnt_send.at[r - 1], recv_sem=cnt_recv.at[r - 1],
            device_id={"elem": lax.rem(me_e + r, ne)}, device_id_type=MESH)

    def kept(i):
        return 2 * lax.rem(mine + i, ways) + core

    def given(i):
        return 2 * lax.rem(mine + i, ways) + 1 - core

    def first_copy(c, i):
        return pltpu.make_async_remote_copy(
            src_ref=part.at[c, given(i)], dst_ref=first.at[c, i],
            send_sem=first_send.at[c, i], recv_sem=first_recv.at[c, i],
            device_id={"elem": partner}, device_id_type=MESH)

    def parts_of(c):
        return SPLIT if c == chunks - 1 else 1

    def rows_of(c, h):
        size = mo // parts_of(c)
        return slice(h * size, (h + 1) * size)

    def second_copy(c, i, h):
        rows = pl.ds(h * (mo // parts_of(c)), mo // parts_of(c))
        return pltpu.make_async_remote_copy(
            src_ref=first.at[c, i, rows], dst_ref=second.at[c, i - 1, rows],
            send_sem=second_send.at[c, i - 1, h], recv_sem=second_recv.at[c, i - 1, h],
            device_id={"elem": kept(i)}, device_id_type=MESH)

    own_in = pltpu.make_async_copy(s_ref, blocks.at[0], s_sem)
    own_in.start()

    barrier = pltpu.get_barrier_semaphore()
    for b in (ahead, behind):
        pl.semaphore_signal(barrier, inc=1, device_id={"beam": b}, device_id_type=MESH)
    for r in range(1, ne):
        pl.semaphore_signal(barrier, inc=1, device_id={"elem": lax.rem(me_e + r, ne)}, device_id_type=MESH)
    pl.semaphore_wait(barrier, 2 + ne - 1)

    arrived = {((0, 0), j) for j in range(q)}
    sent = [0, 0]

    def send_ready():
        for way in (0, 1):
            while sent[way] < len(arrivals[way]):
                d, j = arrivals[way][sent[way]]
                if d > 1 and ((way, d - 1), j) not in arrived:
                    break
                ring_copy(way, d, j).start()
                sent[way] += 1

    send_ready()
    for r in range(1, ne):
        count_copy(r).start()
    for j in range(q):
        for i in (0, 1):
            weight_copy(i, j).start()

    mask[...] = jnp.broadcast_to(flag_ref[...].astype(jnp.float32).astype(jnp.bfloat16), mask.shape)
    own_in.wait()

    sequence = [(0, 0)]
    for d in range(1, half):
        sequence += [(0, d), (1, d)]
    sequence += [(0, half)]

    def members(c):
        return sequence[c * group:(c + 1) * group]

    def stage(c, j):
        for s, (way, d) in enumerate(members(c)):
            columns = pl.ds(j * kq, kq)
            re = blocks[slot_of(way, d), 0, :, columns] * mask[:, columns]
            im = blocks[slot_of(way, d), 1, :, columns] * mask[:, columns]
            lo, hi = s * tb, (group + s) * tb
            rhs[lo:lo + tb, :kq] = re
            rhs[hi:hi + tb, :kq] = im
            rhs[lo:lo + tb, kq:] = -im
            rhs[hi:hi + tb, kq:] = re

    def multiply(c, j, o, fresh):
        rows = pl.ds(pl.multiple_of(o * mo, mo), mo)
        product = lax.dot_general(weights[j, rows, :], rhs[...], (((1,), (1,)), ((), ())),
                                  preferred_element_type=jnp.float32)
        if fresh:
            part[c, o] = product
        else:
            part[c, o] += product

    pieces_done = [0] * chunks
    weights_here = set()
    waiting = []

    def pass_on(c, i):
        first_copy(c, i).wait_recv()
        for h in range(parts_of(c)):
            rows = rows_of(c, h)
            first[c, i, rows] += part[c, kept(i), rows]
            second_copy(c, i, h).start()

    def piece(c, j):
        stage(c, j)
        if j not in weights_here:
            weights_here.add(j)
            for i in (0, 1):
                weight_copy(i, j).wait()
        fresh = pieces_done[c] == 0
        pieces_done[c] += 1
        if pieces_done[c] < q:
            @pl.loop(0, ne)
            def _(o):
                multiply(c, j, o, fresh)
            return
        for i in list(range(1, ways)) + [0]:
            multiply(c, j, given(i), fresh)
            first_copy(c, i).start()
        for i in range(1, ways):
            multiply(c, j, kept(i), fresh)
            if c == chunks - 1:
                pass_on(c, i)
        multiply(c, j, kept(0), fresh)
        if c < chunks - 1:
            waiting.append(c)

    todo = [(c, j) for c in range(chunks) for j in range(q)]

    def run_ready():
        for c, j in list(todo):
            if all((m, j) in arrived for m in members(c)):
                todo.remove((c, j))
                piece(c, j)

    for k in range(len(arrivals[0])):
        for way in (0, 1):
            d, j = arrivals[way][k]
            ring_copy(way, d, j).wait_recv()
            arrived.add(((0 if d == half else way, d), j))
            send_ready()
        for c in waiting:
            for i in range(1, ways):
                pass_on(c, i)
        waiting.clear()
        run_ready()
    for c in waiting:
        for i in range(1, ways):
            pass_on(c, i)
    waiting.clear()

    live = flag_ref[...].astype(jnp.float32)
    for r in range(1, ne):
        count_copy(r).wait()
        live = live + counts[r - 1].astype(jnp.float32)
    gain = jnp.sqrt(jnp.float32(depth * ne) / jnp.sum(live, axis=1, keepdims=True))

    def selection(c):
        column = lax.broadcasted_iota(jnp.int32, (width, 2 * snaps), 0)
        target = lax.broadcasted_iota(jnp.int32, (width, 2 * snaps), 1)
        wanted = column
        for s, (way, d) in enumerate(members(c)):
            source = lookup(order, lax.rem(pos + (d if way else nb - d), nb))
            for p in (0, 1):
                lo = (p * group + s) * tb
                inside = (column >= lo) & (column < lo + tb)
                wanted = jnp.where(inside, column - lo + p * snaps + source * tb, wanted)
        return jnp.where(wanted == target, 1.0, 0.0).astype(jnp.bfloat16)

    def finished(c, h):
        rows = rows_of(c, h)
        value = part[c, me_e, rows] + first[c, 0, rows]
        for i in range(1, ways):
            second_copy(c, i, h).wait_recv()
            value = value + second[c, i - 1, rows]
        return value * gain

    square = jnp.zeros((mo, width), jnp.float32)
    moved = jnp.zeros((mo, 2 * snaps), jnp.float32)
    for c in range(chunks - 1):
        first_copy(c, 0).wait_recv()
        value = finished(c, 0)
        square = square + value * value
        moved = moved + jnp.dot(value.astype(jnp.bfloat16), selection(c), preferred_element_type=jnp.float32)
    c = chunks - 1
    select = selection(c)
    first_copy(c, 0).wait_recv()
    squares = []
    for h in range(SPLIT):
        rows = rows_of(c, h)
        value = finished(c, h)
        squares.append(square[rows] + value * value)
        all_moved = moved[rows] + jnp.dot(value.astype(jnp.bfloat16), select, preferred_element_type=jnp.float32)
        out_ref[0, rows] = all_moved[:, :snaps].astype(jnp.bfloat16)
        out_ref[1, rows] = all_moved[:, snaps:].astype(jnp.bfloat16)
    power = jnp.concatenate([jnp.sum(v, axis=1, keepdims=True) for v in squares], axis=0) * (1.0 / snaps)
    pow_ref[...] = jnp.broadcast_to(power, (mo, LANES)).T[0:1, :]

    for way in (0, 1):
        for d, j in arrivals[way]:
            ring_copy(way, d, j).wait_send()
    for c in range(chunks):
        for i in range(ways):
            first_copy(c, i).wait_send()
        for i in range(1, ways):
            for h in range(parts_of(c)):
                second_copy(c, i, h).wait_send()


def body(order, ne, signals, weights, element_flags):
    nb = len(order)
    _, depth, tb = signals.shape
    rows = weights.shape[1]
    mo = rows // ne
    q = PIECES
    kq = depth // q
    group = min(nb, max(1, LANES // tb))
    chunks = nb // group
    width = 2 * group * tb
    ways = ne // 2
    items = q * (nb // 2) - q // 2
    dma = pltpu.SemaphoreType.DMA
    anywhere = pl.BlockSpec(memory_space=pltpu.MemorySpace.HBM)
    vmem = pl.BlockSpec(memory_space=pltpu.VMEM)
    out, power = pl.pallas_call(
        functools.partial(kernel, order, ne),
        out_shape=(jax.ShapeDtypeStruct((2, mo, nb * tb), jnp.bfloat16),
                   jax.ShapeDtypeStruct((1, mo), jnp.float32)),
        in_specs=[anywhere, vmem, anywhere],
        out_specs=(vmem, vmem),
        scratch_shapes=[
            pltpu.VMEM((nb, 2, tb, depth), jnp.bfloat16),
            pltpu.VMEM((tb, depth), jnp.bfloat16),
            pltpu.VMEM((q, rows, 2 * kq), jnp.bfloat16),
            pltpu.VMEM((width, 2 * kq), jnp.bfloat16),
            pltpu.VMEM((chunks, ne, mo, width), jnp.float32),
            pltpu.VMEM((chunks, ways, mo, width), jnp.float32),
            pltpu.VMEM((chunks, max(1, ways - 1), mo, width), jnp.float32),
            pltpu.VMEM((ne - 1, 1, depth), jnp.int32),
            dma((2, items)), dma((2, items)), dma((2, q)), dma,
            dma((chunks, ways)), dma((chunks, ways)),
            dma((chunks, max(1, ways - 1), SPLIT)), dma((chunks, max(1, ways - 1), SPLIT)),
            dma((ne - 1,)), dma((ne - 1,)),
        ],
        compiler_params=pltpu.CompilerParams(
            collective_id=0, has_side_effects=True, vmem_limit_bytes=50 * 2**20),
        name="beamform",
    )(signals.transpose(0, 2, 1), element_flags.reshape(1, depth), weights)
    return out, power.reshape(mo)


def solution(mesh):
    return jax.shard_map(
        functools.partial(body, ring_order(mesh), mesh.shape["elem"]),
        mesh=mesh,
        in_specs=(P(None, "elem", "beam"), P(None, "beam", "elem"), P("elem")),
        out_specs=(P(None, ("beam", "elem"), None), P(("beam", "elem"))),
        check_vma=False,
    )
```
